32 devices in a mesh: dp: 8 (over z, core), ctx: 4 (over y, x).
Axes of the slice: x: 2, y: 2, z: 4, core: 2. Of those that a mesh axis runs over, the one named last changes fastest.
Arguments:
- queries: bfloat16 [8, 512, 1024], P('dp', 'ctx'), may hold values from -6 to 6
- key_vectors: bfloat16 [8, 512, 1024], P('dp', 'ctx'), may hold values from -6 to 6
- values: bfloat16 [8, 512, 1024], P('dp', 'ctx'), may hold values from -6 to 6
- cotangent: bfloat16 [8, 512, 1024], P('dp', 'ctx'), may hold values from -6 to 6
- lengths: int32 [8], P('dp'), may hold values from 128 to 512
- conv_taps: float32 [31, 1024], replicated, may hold values from -3 to 3
Outputs:
- conv_out: bfloat16 [8, 512, 1024], P('dp', 'ctx')
- query_grad: bfloat16 [8, 512, 1024], P('dp', 'ctx')
- key_grad: bfloat16 [8, 512, 1024], P('dp', 'ctx')
- value_grad: bfloat16 [8, 512, 1024], P('dp', 'ctx')
- taps_grad: float32 [31, 1024], replicated
The draws below stay inside these ranges and needn't reach their ends.
All inputs are finite; a program needn't handle non-finite values.
Results may differ from the reference program's by a relative error of at most 0.024.
Values may be sent and summed in bfloat16 or wider, within the bound.
No kernel may reach another device: no remote copies, remote signals or barrier semaphores. Data moves between devices by JAX's collectives and lax.ppermute only.
A program may use at most 64 MiB of HBM per device.

```python
import jax
import jax.numpy as jnp
from jax import lax

HEADS = 16
HEAD_DIM = 64
KERNEL = 31
D = 1024
FRAMES = 512
UTTS = 8


def base_values(key):
    return jnp.clip(jax.random.normal(key, (UTTS, FRAMES, D), jnp.float32), -6.0, 6.0)


def draw_queries(key, part):
    result = base_values(jax.random.fold_in(key, 1))
    return result.astype(jnp.bfloat16)


def draw_key_vectors(key, part):
    result = base_values(jax.random.fold_in(key, 2))
    return result.astype(jnp.bfloat16)


def place_ends(array, rng, low, largest):
    extent = array.shape
    place = [jax.random.randint(jax.random.fold_in(rng, axis), (), 0, extent[axis]) for axis in range(len(extent))]
    array = array.at[tuple(place)].set(low)
    longest = extent.index(max(extent))
    place[longest] = (place[longest] + 1) % extent[longest]
    return array.at[tuple(place)].set(largest)


def shard_levels(stream_key, dims, pieces, low, high):
    def one(position, parts):
        steps = jax.random.uniform(jax.random.fold_in(jax.random.fold_in(stream_key, 6), position), (parts,), jnp.float32, low / len(pieces), high / len(pieces))
        return jnp.repeat(jnp.exp(steps), dims[position] // parts).reshape((-1,) + (1,) * (len(dims) - position - 1))

    gain = one(*pieces[0])
    for cut in pieces[1:]:
        gain = gain * one(*cut)
    return gain


def bell_draw(key, extent, spread, bound, split=(), kind=jnp.bfloat16):
    entries = jax.random.normal(key, extent, jnp.float32) * spread
    if len(split) > 0:
        entries = shard_levels(key, extent, split, -0.22, 0.18) * entries
    return jnp.clip(entries, min=-bound, max=bound).astype(kind)


def setup_inputs(seed: int = 0) -> dict:
    arg_keys = jax.random.split(jax.random.key(seed), 7)
    return {
        "queries": draw_queries(jax.random.fold_in(arg_keys[6], 71), 0),
        "key_vectors": draw_key_vectors(jax.random.fold_in(arg_keys[6], 71), 0),
        "values": bell_draw(arg_keys[2], (UTTS, FRAMES, D), 1.0, 6.0, ((0, 8), (1, 4))),
        "cotangent": bell_draw(arg_keys[3], (UTTS, FRAMES, D), 1.0, 6.0, ((0, 8), (1, 4))),
        "lengths": place_ends(jax.random.randint(arg_keys[4], (UTTS,), FRAMES // 4, FRAMES + 1), jax.random.fold_in(arg_keys[4], 1), FRAMES // 4, FRAMES).astype(jnp.int32),
        "conv_taps": bell_draw(arg_keys[5], (KERNEL, D), 0.5, 3.0, (), jnp.float32),
    }


def masked_scores(query_head, key_head, valid_keys):
    scores = jnp.dot(query_head, key_head.T, preferred_element_type=jnp.float32) * (HEAD_DIM ** -0.5)
    return jnp.where(valid_keys[None, :], scores, -1e30)


def per_utterance(operands, conv_taps):
    queries, key_vectors, values, cotangent, length = operands
    half_width = KERNEL // 2
    score_scale = HEAD_DIM ** -0.5
    positions = jnp.arange(FRAMES, dtype=jnp.int32)
    valid_keys = positions < length
    query_heads = queries.reshape(FRAMES, HEADS, HEAD_DIM).transpose(1, 0, 2)
    key_heads = key_vectors.reshape(FRAMES, HEADS, HEAD_DIM).transpose(1, 0, 2)
    value_heads = values.reshape(FRAMES, HEADS, HEAD_DIM).transpose(1, 0, 2)

    def forward_head(head_ops):
        query_head, key_head, value_head = head_ops
        scores = masked_scores(query_head, key_head, valid_keys)
        row_top = jnp.max(scores, axis=1, keepdims=True)
        log_total = row_top + jnp.log(jnp.sum(jnp.exp(scores - row_top), axis=1, keepdims=True))
        softmax_bf = jnp.exp(scores - log_total).astype(jnp.bfloat16)
        attended = jnp.dot(softmax_bf, value_head, preferred_element_type=jnp.float32).astype(jnp.bfloat16)
        return attended, log_total[:, 0]

    attended_heads, log_totals = lax.map(forward_head, (query_heads, key_heads, value_heads))
    merged = attended_heads.transpose(1, 0, 2).reshape(FRAMES, D)
    kept = jnp.where(valid_keys[:, None], merged, jnp.zeros_like(merged))
    padded_in = jnp.pad(kept.astype(jnp.float32), ((half_width, half_width), (0, 0)))
    padded_cot = jnp.pad(cotangent.astype(jnp.float32), ((half_width, half_width), (0, 0)))
    cot_rows = cotangent.astype(jnp.float32)
    conv_sum = jnp.zeros((FRAMES, D), jnp.float32)
    back_sum = jnp.zeros((FRAMES, D), jnp.float32)
    tap_rows = []
    for tap_index in range(KERNEL):
        window = padded_in[tap_index:tap_index + FRAMES]
        conv_sum = conv_sum + conv_taps[tap_index] * window
        back_sum = back_sum + conv_taps[tap_index] * padded_cot[2 * half_width - tap_index:2 * half_width - tap_index + FRAMES]
        tap_rows.append(jnp.sum(cot_rows * window, axis=0))
    conv_out = conv_sum.astype(jnp.bfloat16)
    taps_part = jnp.stack(tap_rows)
    attended_grad = jnp.where(valid_keys[:, None], back_sum, jnp.zeros_like(back_sum)).astype(jnp.bfloat16)
    grad_heads = attended_grad.reshape(FRAMES, HEADS, HEAD_DIM).transpose(1, 0, 2)

    def backward_head(head_ops):
        query_head, key_head, value_head, out_head, grad_head, log_total = head_ops
        scores = masked_scores(query_head, key_head, valid_keys)
        softmax = jnp.exp(scores - log_total[:, None])
        row_delta = jnp.sum(grad_head.astype(jnp.float32) * out_head.astype(jnp.float32), axis=1)
        prob_grad = jnp.dot(grad_head, value_head.T, preferred_element_type=jnp.float32)
        score_grad = (softmax * (prob_grad - row_delta[:, None])).astype(jnp.bfloat16)
        query_grad = (jnp.dot(score_grad, key_head, preferred_element_type=jnp.float32) * score_scale).astype(jnp.bfloat16)
        key_grad = (jnp.dot(score_grad.T, query_head, preferred_element_type=jnp.float32) * score_scale).astype(jnp.bfloat16)
        value_grad = jnp.dot(softmax.astype(jnp.bfloat16).T, grad_head, preferred_element_type=jnp.float32).astype(jnp.bfloat16)
        return query_grad, key_grad, value_grad

    query_grad, key_grad, value_grad = lax.map(backward_head, (query_heads, key_heads, value_heads, attended_heads, grad_heads, log_totals))

    def merge_heads(head_array):
        return head_array.transpose(1, 0, 2).reshape(FRAMES, D)

    return conv_out, merge_heads(query_grad), merge_heads(key_grad), merge_heads(value_grad), taps_part


def reference(queries, key_vectors, values, cotangent, lengths, conv_taps):
    def one_utterance(operands):
        return per_utterance(operands, conv_taps)

    conv_out, query_grad, key_grad, value_grad, taps_parts = lax.map(one_utterance, (queries, key_vectors, values, cotangent, lengths))
    taps_grad = jnp.sum(taps_parts, axis=0)
    return (conv_out, query_grad, key_grad, value_grad, taps_grad)
```

```python
import functools

import jax
import jax.numpy as jnp
from jax import lax
from jax.experimental import pallas as pl
from jax.experimental.pallas import tpu as pltpu
from jax.sharding import PartitionSpec as P

HEAD_DIM = 64
KERNEL = 31
HALF = KERNEL // 2
LANES = 128
EDGE = 16
ROW_BLOCK = 64


VMEM = pl.BlockSpec(memory_space=pltpu.VMEM)
SMEM = pl.BlockSpec(memory_space=pltpu.SMEM)
ANY = pl.BlockSpec(memory_space=pl.ANY)


def pack_kernel(peers, where_ref, a_ref, b_ref, *out_refs):
    width = out_refs[0].shape[2]
    for step in range(1, peers):
        cols = pl.ds(pl.multiple_of((where_ref[0] ^ step) * width, LANES), width)
        out_refs[step - 1][0] = a_ref[:, cols]
        out_refs[step - 1][1] = b_ref[:, cols]


def pack(where, first, second, peers):
    rows, width = first.shape
    block = jax.ShapeDtypeStruct((2, rows, width // peers), first.dtype)
    return pl.pallas_call(
        functools.partial(pack_kernel, peers),
        out_shape=[block] * (peers - 1),
        in_specs=[SMEM, VMEM, VMEM],
        out_specs=[VMEM] * (peers - 1),
    )(where, first, second)


def unpack_kernel(peers, where_ref, *refs):
    in_refs = refs[:peers]
    tap_refs = refs[peers : 2 * peers]
    out_refs = refs[2 * peers : 2 * peers + 4]
    taps_ref = refs[2 * peers + 4]
    width = in_refs[0].shape[2]
    for step in range(peers):
        cols = pl.ds(pl.multiple_of((where_ref[0] ^ step) * width, LANES), width)
        for which in range(4):
            out_refs[which][:, cols] = in_refs[step][which]
        taps_ref[:, cols] = tap_refs[step][:KERNEL]


def unpack(where, blocks, taps, peers):
    _, rows, width = blocks[0].shape
    return pl.pallas_call(
        functools.partial(unpack_kernel, peers),
        out_shape=[jax.ShapeDtypeStruct((rows, peers * width), jnp.bfloat16)] * 4
        + [jax.ShapeDtypeStruct((KERNEL, peers * width), jnp.float32)],
        in_specs=[SMEM] + [VMEM] * (2 * peers),
        out_specs=[VMEM] * 5,
    )(where, *blocks, *taps)


def nt_dot(left, right):
    return lax.dot_general(
        left, right, (((1,), (1,)), ((), ())), preferred_element_type=jnp.float32
    )


def nn_dot(left, right):
    return jnp.dot(left, right, preferred_element_type=jnp.float32)


def core_kernel(peers, where_ref, length_ref, *refs):
    own = refs[:4]
    first_in = refs[4 : 3 + peers]
    second_in = refs[3 + peers : 2 + 2 * peers]
    taps_ref = refs[2 + 2 * peers]
    outs = refs[3 + 2 * peers : 3 + 3 * peers]
    tap_out = refs[3 + 3 * peers]
    q_s, k_s, v_s, g_s, res, cot_pad, kept_pad, tap_acc, sems = refs[4 + 3 * peers :]
    me = where_ref[0]
    length = length_ref[0]
    rows = own[0].shape[0]
    width = own[0].shape[1]
    frames = rows * peers
    tiles = width // LANES
    row_blocks = frames // ROW_BLOCK

    for tile in range(tiles):
        zero_edge = jnp.zeros((EDGE, LANES), jnp.float32)
        for pad in (cot_pad, kept_pad):
            pad[tile, :EDGE] = zero_edge
            pad[tile, EDGE + frames :] = zero_edge
    for step in range(peers):
        start = pl.multiple_of((me ^ step) * rows, LANES)
        place = pl.ds(start, rows)
        if step == 0:
            q_part, k_part, v_part, c_part = (own[i][...] for i in range(4))
        else:
            q_part, k_part = first_in[step - 1][0], first_in[step - 1][1]
            v_part, c_part = second_in[step - 1][0], second_in[step - 1][1]
        q_s[place] = q_part * jnp.bfloat16(HEAD_DIM**-0.5)
        k_s[place] = k_part
        v_s[place] = v_part
        for tile in range(tiles):
            cot_pad[tile, pl.ds(start + EDGE, rows)] = c_part[
                :, tile * LANES : (tile + 1) * LANES
            ].astype(jnp.float32)

    def tap_row(tile, index):
        return taps_ref[index : index + 1, tile * LANES : (tile + 1) * LANES]

    row_iota = lax.broadcasted_iota(jnp.int32, (ROW_BLOCK, LANES), 0)
    for tile in range(tiles):
        cols = slice(tile * LANES, (tile + 1) * LANES)

        def back_block(index, carry):
            base = pl.multiple_of(index * ROW_BLOCK, ROW_BLOCK)
            total = jnp.zeros((ROW_BLOCK, LANES), jnp.float32)
            for tap in range(KERNEL):
                total = (
                    total
                    + tap_row(tile, tap)
                    * cot_pad[tile, pl.ds(base + (EDGE + HALF - tap), ROW_BLOCK)]
                )
            total = jnp.where(row_iota + base < length, total, 0.0)
            g_s[pl.ds(base, ROW_BLOCK), cols] = total.astype(jnp.bfloat16)
            return carry

        lax.fori_loop(0, row_blocks, back_block, 0)

    lane = lax.broadcasted_iota(jnp.int32, (frames, LANES), 1)
    key_pos = lax.broadcasted_iota(jnp.int32, (frames, LANES), 0)
    in_head = [lane < HEAD_DIM, lane >= HEAD_DIM]
    spare = [lane == HEAD_DIM, lane == 0]
    zero_bf = jnp.zeros((frames, LANES), jnp.bfloat16)
    one_bf = jnp.ones((frames, LANES), jnp.bfloat16)
    bias = jnp.where(key_pos < length, 0.0, -1e30).astype(jnp.bfloat16)
    query_pos = lax.broadcasted_iota(jnp.int32, (LANES, frames), 1)

    for tile in range(tiles):
        cols = slice(tile * LANES, (tile + 1) * LANES)
        q_t = q_s[:, cols]
        k_t = k_s[:, cols]
        v_t = v_s[:, cols]
        g_t = g_s[:, cols]
        v_tr = v_t.T
        k_tr = k_t.T
        g_tr = g_t.T.astype(jnp.float32)
        out_tr, dq_tr = [], []
        dv = dk = None
        for head in range(2):
            half = slice(head * HEAD_DIM, (head + 1) * HEAD_DIM)
            q_h = jnp.where(in_head[head], q_t, zero_bf)
            g_h = jnp.where(in_head[head], g_t, zero_bf)
            q_aug = jnp.where(spare[head], one_bf, q_h)
            k_aug = jnp.where(in_head[head], k_t, jnp.where(spare[head], bias, zero_bf))
            scores = nt_dot(k_aug, q_aug)
            top = jnp.max(scores, axis=0, keepdims=True)
            grown = jnp.exp(scores - top)
            soft = grown * (1.0 / jnp.sum(grown, axis=0, keepdims=True))
            soft_bf = soft.astype(jnp.bfloat16)
            out_h = nn_dot(v_tr[half], soft_bf).astype(jnp.bfloat16).astype(jnp.float32)
            out_tr.append(out_h)
            delta = jnp.sum(out_h * g_tr[half], axis=0, keepdims=True)
            prob = nt_dot(v_t, g_h)
            score_grad = (soft * (prob - delta)).astype(jnp.bfloat16)
            dq_tr.append(nn_dot(k_tr[half], score_grad) * (HEAD_DIM**-0.5))
            dv_h = nn_dot(soft_bf, g_h)
            dk_h = nn_dot(score_grad, q_h)
            dv = dv_h if dv is None else dv + dv_h
            dk = dk_h if dk is None else dk + dk_h
        out_pair = jnp.concatenate(out_tr, axis=0)
        out_pair = jnp.where(query_pos < length, out_pair, 0.0)
        kept_pad[tile, EDGE : EDGE + frames] = out_pair.T
        res[1, :, cols] = jnp.concatenate(dq_tr, axis=0).T.astype(jnp.bfloat16)
        res[2, :, cols] = dk.astype(jnp.bfloat16)
        res[3, :, cols] = dv.astype(jnp.bfloat16)

    for tile in range(tiles):
        cols = slice(tile * LANES, (tile + 1) * LANES)
        tap_acc[...] = jnp.zeros_like(tap_acc)

        def conv_block(index, carry):
            base = pl.multiple_of(index * ROW_BLOCK, ROW_BLOCK)
            total = jnp.zeros((ROW_BLOCK, LANES), jnp.float32)
            cot = cot_pad[tile, pl.ds(base + EDGE, ROW_BLOCK)]
            for tap in range(KERNEL):
                window = kept_pad[tile, pl.ds(base + (EDGE - HALF + tap), ROW_BLOCK)]
                total = total + tap_row(tile, tap) * window
                tap_acc[tap] += jnp.sum((cot * window).reshape(-1, 8, LANES), axis=0)
            res[0, pl.ds(base, ROW_BLOCK), cols] = total.astype(jnp.bfloat16)
            return carry

        lax.fori_loop(0, row_blocks, conv_block, 0)
        tap_out[:, cols] = jnp.sum(tap_acc[...], axis=1)

    copies = []
    for step in range(peers):
        start = pl.multiple_of((me ^ step) * rows, LANES)
        copies.append(
            pltpu.make_async_copy(res.at[:, pl.ds(start, rows)], outs[step], sems.at[step])
        )
        copies[-1].start()
    for copy in copies:
        copy.wait()


def core(where, length, own, first_in, second_in, conv_taps, peers):
    rows, full = own[0].shape
    width = full // peers
    frames = rows * peers
    tiles = width // LANES
    pair = pl.BlockSpec((2, rows, width), lambda i, w, n: (0, 0, 0))
    mine = pl.BlockSpec((rows, width), lambda i, w, n: (0, w[0]))
    grid_spec = pltpu.PrefetchScalarGridSpec(
        num_scalar_prefetch=2,
        grid=(1,),
        in_specs=[mine] * 4
        + [pair] * (2 * (peers - 1))
        + [pl.BlockSpec((KERNEL, width), lambda i, w, n: (0, w[0]))],
        out_specs=[ANY] * peers + [pl.BlockSpec((KERNEL + 1, width), lambda i, w, n: (0, 0))],
        scratch_shapes=[pltpu.VMEM((frames, width), jnp.bfloat16)] * 4
        + [
            pltpu.VMEM((4, frames, width), jnp.bfloat16),
            pltpu.VMEM((tiles, frames + 2 * EDGE, LANES), jnp.float32),
            pltpu.VMEM((tiles, frames + 2 * EDGE, LANES), jnp.float32),
            pltpu.VMEM((KERNEL + 1, 8, LANES), jnp.float32),
            pltpu.SemaphoreType.DMA((peers,)),
        ],
    )
    return pl.pallas_call(
        functools.partial(core_kernel, peers),
        out_shape=[jax.ShapeDtypeStruct((4, rows, width), jnp.bfloat16)] * peers
        + [jax.ShapeDtypeStruct((KERNEL + 1, width), jnp.float32)],
        grid_spec=grid_spec,
        compiler_params=pltpu.CompilerParams(vmem_limit_bytes=48 * 2**20),
    )(where, length, *own, *first_in, *second_in, conv_taps)


def swap(array, axis, bits):
    count = lax.axis_size(axis)
    return lax.ppermute(array, axis, [(i, i ^ bits) for i in range(count)])


def by_heads(queries, key_vectors, values, cotangent, lengths, conv_taps):
    peers = lax.axis_size("ctx")
    groups = lax.axis_size("dp")
    if queries.shape[2] // peers % LANES != 0:
        return by_heads_native(queries, key_vectors, values, cotangent, lengths, conv_taps)
    where = lax.axis_index("ctx").astype(jnp.int32).reshape(1)
    own = (queries[0], key_vectors[0], values[0], cotangent[0])
    steps = range(1, peers)
    first_out = pack(where, own[0], own[1], peers)
    first_in = [swap(first_out[step - 1], "ctx", step) for step in steps]
    second_out = pack(where, own[2], own[3], peers)
    second_in = [swap(second_out[step - 1], "ctx", step) for step in steps]
    *blocks, taps = core(where, lengths, own, first_in, second_in, conv_taps, peers)
    back = [blocks[0]] + [swap(blocks[step], "ctx", step) for step in steps]
    taps = taps + swap(taps, "dp", 1)
    taps = taps + sum(swap(taps, "dp", 2 * step) for step in range(1, groups // 2))
    tap_blocks = [taps] + [swap(taps, "ctx", step) for step in steps]
    conv_out, query_grad, key_grad, value_grad, taps_grad = unpack(
        where, back, tap_blocks, peers
    )
    return (conv_out[None], query_grad[None], key_grad[None], value_grad[None], taps_grad)


def split_heads(flat_rows):
    return flat_rows.reshape(flat_rows.shape[0], flat_rows.shape[1] // HEAD_DIM, HEAD_DIM)


def native_forward(query_heads, key_heads, value_heads, valid_keys, block_rows):
    score_scale = HEAD_DIM ** (-0.5)

    def one_block(query_part):
        scores = (
            jnp.einsum("qhd,khd->hqk", query_part, key_heads, preferred_element_type=jnp.float32)
            * score_scale
        )
        scores = jnp.where(valid_keys[None, None, :], scores, -1e30)
        row_top = jnp.max(scores, axis=2, keepdims=True)
        log_total = row_top + jnp.log(jnp.sum(jnp.exp(scores - row_top), axis=2, keepdims=True))
        softmax_bf = jnp.exp(scores - log_total).astype(jnp.bfloat16)
        attended = jnp.einsum(
            "hqk,khd->qhd", softmax_bf, value_heads, preferred_element_type=jnp.float32
        ).astype(jnp.bfloat16)
        return (attended, log_total[:, :, 0])

    blocked = query_heads.reshape(-1, block_rows, *query_heads.shape[1:])
    attended, log_totals = lax.map(one_block, blocked)
    return (attended.reshape(query_heads.shape), log_totals)


def native_backward(
    query_heads, key_heads, value_heads, out_heads, grad_heads, log_totals, valid_keys, block_rows
):
    score_scale = HEAD_DIM ** (-0.5)

    def one_block(carried, inputs):
        query_part, out_part, grad_part, log_part = inputs
        key_acc, value_acc = carried
        scores = (
            jnp.einsum("qhd,khd->hqk", query_part, key_heads, preferred_element_type=jnp.float32)
            * score_scale
        )
        scores = jnp.where(valid_keys[None, None, :], scores, -1e30)
        softmax = jnp.exp(scores - log_part[:, :, None])
        row_delta = jnp.sum(grad_part.astype(jnp.float32) * out_part.astype(jnp.float32), axis=2).T
        prob_grad = jnp.einsum(
            "qhd,khd->hqk", grad_part, value_heads, preferred_element_type=jnp.float32
        )
        score_grad = (softmax * (prob_grad - row_delta[:, :, None])).astype(jnp.bfloat16)
        query_grad = (
            jnp.einsum("hqk,khd->qhd", score_grad, key_heads, preferred_element_type=jnp.float32)
            * score_scale
        ).astype(jnp.bfloat16)
        key_acc = key_acc + jnp.einsum(
            "hqk,qhd->khd", score_grad, query_part, preferred_element_type=jnp.float32
        )
        value_acc = value_acc + jnp.einsum(
            "hqk,qhd->khd",
            softmax.astype(jnp.bfloat16),
            grad_part,
            preferred_element_type=jnp.float32,
        )
        return ((key_acc, value_acc), query_grad)

    zeros_acc = jnp.zeros(key_heads.shape, jnp.float32)
    blocked = [
        part.reshape(-1, block_rows, *part.shape[1:])
        for part in (query_heads, out_heads, grad_heads)
    ]
    (key_acc, value_acc), query_grad = lax.scan(
        one_block, (zeros_acc, zeros_acc), (*blocked, log_totals)
    )
    key_grad = (key_acc * score_scale).astype(jnp.bfloat16)
    return (query_grad.reshape(query_heads.shape), key_grad, value_acc.astype(jnp.bfloat16))


def native_conv(kept, cotangent, conv_taps, valid_rows):
    frames = kept.shape[0]
    margins = ((HALF, HALF), (0, 0))
    padded_in = jnp.pad(kept.astype(jnp.float32), margins)
    padded_cot = jnp.pad(cotangent.astype(jnp.float32), margins)
    cot_rows = cotangent.astype(jnp.float32)
    conv_sum = jnp.zeros(kept.shape, jnp.float32)
    back_sum = jnp.zeros(kept.shape, jnp.float32)
    tap_rows = []
    for tap in range(KERNEL):
        window = padded_in[tap : tap + frames]
        conv_sum = conv_sum + conv_taps[tap] * window
        back_sum = back_sum + conv_taps[tap] * padded_cot[2 * HALF - tap : 2 * HALF - tap + frames]
        tap_rows.append(jnp.sum(cot_rows * window, axis=0))
    grad = jnp.where(valid_rows[:, None], back_sum, 0.0)
    return (conv_sum.astype(jnp.bfloat16), grad.astype(jnp.bfloat16), jnp.stack(tap_rows))


def by_heads_native(queries, key_vectors, values, cotangent, lengths, conv_taps):
    stacked = jnp.stack([queries[0], key_vectors[0], values[0], cotangent[0]])
    exchanged = lax.all_to_all(stacked, "ctx", split_axis=2, concat_axis=1, tiled=True)
    frames, width = exchanged.shape[1:]
    block_rows = min(512, frames)
    valid = jnp.arange(frames, dtype=jnp.int32) < lengths[0]
    heads = [split_heads(exchanged[which]) for which in range(3)]
    out_heads, log_totals = native_forward(*heads, valid, block_rows)
    kept = jnp.where(valid[:, None], out_heads.reshape(frames, width), jnp.bfloat16(0))
    my_taps = lax.dynamic_slice_in_dim(conv_taps, lax.axis_index("ctx") * width, width, 1)
    conv_out, grad, taps_part = native_conv(kept, exchanged[3], my_taps, valid)
    grads = native_backward(
        *heads, out_heads, split_heads(grad), log_totals, valid, block_rows
    )
    results = jnp.stack([conv_out] + [part.reshape(frames, width) for part in grads])
    results = lax.all_to_all(results, "ctx", split_axis=1, concat_axis=2, tiled=True)
    taps = lax.all_gather(lax.psum(taps_part, "dp"), "ctx", axis=1, tiled=True)
    return (*(results[which][None] for which in range(4)), taps)


def solution(mesh):
    spec = P("dp", "ctx", None)
    return jax.shard_map(
        by_heads,
        mesh=mesh,
        in_specs=(spec, spec, spec, spec, P("dp"), P()),
        out_specs=(spec, spec, spec, spec, P()),
        check_vma=False,
    )
```
